32 devices in a mesh: sub: 4 (over x, core), tile: 8 (over z, y).
Axes of the slice: x: 2, y: 2, z: 4, core: 2. Of those that a mesh axis runs over, the one named last changes fastest.
Arguments:
- states: float32 [4, 3, 256, 2048], P('sub', None, 'tile'), may hold values from -6 to 6
- terrain: int32 [256, 2048], P('tile'), may hold values from 0 to 7
- depth_table: float32 [8], replicated, may hold values from 0.5 to 2
- spread_table: float32 [8], replicated, may hold values from 0.03 to 0.24
- mixing: float32 [4, 4], replicated, may hold values from -0.9 to 2, as said below
Outputs:
- gradient: float32 [4, 3, 256, 2048], P('sub', None, 'tile')
The draws below stay inside these ranges and needn't reach their ends.
Inputs may be any that keep to these rules, and one draw needn't show every extreme that they name: `mixing`: A dense matrix with diagonal entries between 1 and 2.
All inputs are finite; a program needn't handle non-finite values.
Results may differ from the reference program's by a relative error of at most 0.00012.
Values sent between devices are 32-bit elements; how exact they have to be, the bound alone decides.
A program may use at most 64 MiB of HBM per device.

```python
import math
import jax
import jax.numpy as jnp
from jax import lax

NY = 2048
NCLASS = 8
FSTEPS = 3
DSTEPS = 3
S = 4
NX = 256


def draw_mixing(key, part):
    first_key = jax.random.fold_in(key, 11)
    second_key = jax.random.fold_in(key, 12)
    diagonal = jax.random.uniform(first_key, (S,), jnp.float32, 1.0, 2.0)
    off = jnp.clip(0.3 * jax.random.normal(second_key, (S, S), jnp.float32), -0.9, 0.9)
    eye = jnp.eye(S, dtype=jnp.float32)
    return off * (1.0 - eye) + eye * diagonal[None, :]


def touch_ends(entries, stream_key, smallest, largest):
    longest = entries.shape.index(max(entries.shape))
    spots = []
    for shift in (0, 1):
        where = [jax.random.randint(jax.random.fold_in(stream_key, axis), (), 0, length) for axis, length in enumerate(entries.shape)]
        where[longest] = (where[longest] + shift) % entries.shape[longest]
        spots.append(tuple(where))
    return entries.at[spots[0]].set(smallest).at[spots[1]].set(largest)


def steps_of(rng, extent, cuts, smallest, largest):
    def one(position, blocks):
        heights = jax.random.uniform(jax.random.fold_in(jax.random.fold_in(rng, 6), position), (blocks,), jnp.float32, smallest / len(cuts), largest / len(cuts))
        return jnp.repeat(jnp.exp(heights), extent[position] // blocks).reshape((-1,) + (1,) * (len(extent) - position - 1))

    gain = one(*cuts[0])
    for cut in cuts[1:]:
        gain = gain * one(*cut)
    return gain


def scatter_about(rng, shape, width, bound, shards=(), kind=jnp.bfloat16):
    entries = jax.random.normal(rng, shape, jnp.float32) * width
    if len(shards) > 0:
        entries = steps_of(rng, shape, shards, -0.22, 0.18) * entries
    return jnp.clip(entries, min=-bound, max=bound).astype(kind)


def setup_inputs(seed: int = 0) -> dict:
    keys = jax.random.split(jax.random.key(seed), 6)
    return {
        "states": scatter_about(keys[0], (S, 3, NX, NY), 1.0, 6.0, ((0, 4), (2, 8)), jnp.float32),
        "terrain": touch_ends(jax.random.randint(keys[1], (NX, NY), 0, NCLASS), jax.random.fold_in(keys[1], 1), 0, NCLASS - 1).astype(jnp.int32),
        "depth_table": jnp.clip(jnp.exp(jax.random.uniform(keys[2], (NCLASS,), jnp.float32, math.log(0.5), math.log(2.0))), 0.5, 2.0),
        "spread_table": jnp.clip(jax.random.uniform(keys[3], (NCLASS,), jnp.float32, 0.03, 0.24), 0.03, 0.24),
        "mixing": draw_mixing(jax.random.fold_in(keys[5], 71), 0),
    }


time_step = 0.5
gravity = 1.0
coriolis = 0.3


def col_diff(field):
    return (jnp.roll(field, -1, -1) - jnp.roll(field, 1, -1)) * 0.5


def row_mask(first, count, total):
    index = first + jnp.arange(count, dtype=jnp.int32)
    return ((index >= 0) & (index < total)).astype(jnp.float32)[:, None]


def model_step(state, depth, first, total):
    height, east, north = state[0], state[1], state[2]
    flux_x = depth * east
    flux_y = depth * north
    new_h = height[1:-1] - time_step * ((flux_x[2:] - flux_x[:-2]) * 0.5 + col_diff(flux_y[1:-1]))
    new_h = new_h * row_mask(first + 1, new_h.shape[0], total)
    new_u = east[2:-2] - time_step * gravity * (new_h[2:] - new_h[:-2]) * 0.5 + time_step * coriolis * north[2:-2]
    new_v = north[2:-2] - time_step * gravity * col_diff(new_h[1:-1]) - time_step * coriolis * east[2:-2]
    result = jnp.stack([new_h[1:-1], new_u, new_v])
    return result * row_mask(first + 2, result.shape[1], total)


def spread_step(field, kappa, first, total):
    centre = field[:, 1:-1]
    laplace = field[:, 2:] + field[:, :-2] + jnp.roll(centre, 1, 2) + jnp.roll(centre, -1, 2) - 4.0 * centre
    return (centre + kappa * laplace) * row_mask(first + 1, centre.shape[1], total)


def reference(states, terrain, depth_table, spread_table, mixing):
    classes = jnp.arange(NCLASS, dtype=jnp.int32)
    pick = (terrain[None] == classes[:, None, None]).astype(jnp.float32)
    depth = jnp.sum(pick * depth_table[:, None, None], 0)
    kappa = jnp.sum(pick * spread_table[:, None, None], 0)
    depth_pad = jnp.pad(depth, ((2, 2), (0, 0)))

    def forward(state):
        for step in range(FSTEPS):
            padded = jnp.pad(state, ((0, 0), (2, 2), (0, 0)))
            state = model_step(padded, depth_pad, -2, NX)
        return state

    ends = lax.map(forward, states)
    earlier = jnp.concatenate([jnp.zeros_like(ends[:1]), ends[:-1]], 0)
    jumps = states - earlier
    mixed = jnp.einsum("st,tfxy->sfxy", mixing, jumps, precision=lax.Precision.HIGHEST)

    def smooth(field):
        for step in range(DSTEPS):
            padded = jnp.pad(field, ((0, 0), (1, 1), (0, 0)))
            field = spread_step(padded, kappa, -1, NX)
        return field

    return lax.map(smooth, mixed)
```

```python
import functools

import jax
import jax.numpy as jnp
from jax import lax
from jax.experimental import pallas as pl
from jax.experimental.pallas import tpu as pltpu
from jax.sharding import PartitionSpec as P

FSTEPS = 3
DSTEPS = 3
time_step = 0.5
gravity = 1.0
coriolis = 0.3

PAD = 8
LANES = 128
FHALO = 2 * FSTEPS
CHUNK = 512


def kernel(
    subs, tiles, rows, cols, nclass,
    states, terrain, depth_tab, spread_tab, mixing, out,
    S, T, D, K, send_a, recv_a, send_b, recv_b, M,
    load_sem, halo_send, halo_recv, a_send, a_recv, b_send, b_recv, m_send, m_recv,
):
    pairs = subs // 2
    nch = cols // CHUNK
    me = lax.axis_index("sub")
    tile = lax.axis_index("tile")
    parity = lax.rem(me, 2)
    mate = me + 1 - 2 * parity
    pair = me // 2
    has_up = tile > 0
    has_down = tile < tiles - 1
    up, down = tile - 1, tile + 1

    loads = [
        pltpu.make_async_copy(states.at[0], S.at[:, pl.ds(PAD, rows), :], load_sem.at[0]),
        pltpu.make_async_copy(terrain, T.at[pl.ds(PAD, rows), :], load_sem.at[1]),
    ]
    for copy in loads:
        copy.start()

    barrier = pltpu.get_barrier_semaphore()
    pl.semaphore_signal(barrier, inc=1, device_id={"sub": mate})
    for k in range(1, pairs):
        pl.semaphore_signal(
            barrier, inc=1, device_id={"sub": lax.rem(pair + k, pairs) * 2 + parity}
        )

    @pl.when(has_up)
    def _():
        pl.semaphore_signal(barrier, inc=1, device_id={"tile": up})

    @pl.when(has_down)
    def _():
        pl.semaphore_signal(barrier, inc=1, device_id={"tile": down})

    pl.semaphore_wait(
        barrier, pairs + has_up.astype(jnp.int32) + has_down.astype(jnp.int32)
    )

    def halo_copy(source, target, index, where):
        return pltpu.make_async_remote_copy(
            src_ref=source, dst_ref=target, send_sem=halo_send.at[index],
            recv_sem=halo_recv.at[index], device_id={"tile": where},
            device_id_type=pl.DeviceIdType.MESH,
        )

    last, first = pl.ds(rows - FHALO, FHALO), pl.ds(0, FHALO)
    above, below = pl.ds(PAD - FHALO, FHALO), pl.ds(PAD + rows, FHALO)
    to_down = [
        halo_copy(terrain.at[last, :], T.at[above, :], 0, down),
        halo_copy(states.at[0, :, last, :], S.at[:, above, :], 1, down),
    ]
    to_up = [
        halo_copy(terrain.at[first, :], T.at[below, :], 2, up),
        halo_copy(states.at[0, :, first, :], S.at[:, below, :], 3, up),
    ]

    @pl.when(has_down)
    def _():
        for copy in to_down:
            copy.start()

    @pl.when(has_up)
    def _():
        for copy in to_up:
            copy.start()

    S[:, 0:PAD - FHALO, :] = jnp.zeros((3, PAD - FHALO, cols), jnp.float32)
    T[0:PAD - FHALO, :] = jnp.full((PAD - FHALO, cols), -1, jnp.int32)
    S[:, PAD + rows + FHALO:, :] = jnp.zeros((3, PAD - FHALO, cols), jnp.float32)
    T[PAD + rows + FHALO:, :] = jnp.full((PAD - FHALO, cols), -1, jnp.int32)
    M[:, 0:PAD - DSTEPS, :] = jnp.zeros((3, PAD - DSTEPS, cols), jnp.float32)
    M[:, PAD + rows + DSTEPS:, :] = jnp.zeros((3, PAD - DSTEPS, cols), jnp.float32)

    @pl.when(jnp.logical_not(has_up))
    def _():
        S[:, PAD - FHALO:PAD, :] = jnp.zeros((3, FHALO, cols), jnp.float32)
        T[PAD - FHALO:PAD, :] = jnp.full((FHALO, cols), -1, jnp.int32)
        M[:, PAD - DSTEPS:PAD, :] = jnp.zeros((3, DSTEPS, cols), jnp.float32)

    @pl.when(jnp.logical_not(has_down))
    def _():
        S[:, PAD + rows:PAD + rows + FHALO, :] = jnp.zeros((3, FHALO, cols), jnp.float32)
        T[PAD + rows:PAD + rows + FHALO, :] = jnp.full((FHALO, cols), -1, jnp.int32)
        M[:, PAD + rows:PAD + rows + DSTEPS, :] = jnp.zeros((3, DSTEPS, cols), jnp.float32)

    def lookup(start, count):
        for c in range(nch):
            span = pl.ds(c * CHUNK, CHUNK)
            kind = T[pl.ds(start, count), span]
            depth = jnp.zeros(kind.shape, jnp.float32)
            kappa = jnp.zeros(kind.shape, jnp.float32)
            for n in range(nclass):
                hit = kind == n
                depth = jnp.where(hit, depth_tab[n], depth)
                kappa = jnp.where(hit, spread_tab[n], kappa)
            D[pl.ds(start, count), span] = depth
            K[pl.ds(start, count), span] = kappa

    for copy in loads:
        copy.wait()
    lookup(PAD, rows)

    def wide(ref, lead, start, count, c):
        before = (c * CHUNK - LANES) % cols
        after = ((c + 1) * CHUNK) % cols
        return jnp.concatenate(
            [
                ref[lead + (pl.ds(start, count), pl.ds(before, LANES))],
                ref[lead + (pl.ds(start, count), pl.ds(c * CHUNK, CHUNK))],
                ref[lead + (pl.ds(start, count), pl.ds(after, LANES))],
            ],
            axis=-1,
        )

    def nxt(value, axis):
        return pltpu.roll(value, value.shape[axis] - 1, axis)

    def prv(value, axis):
        return pltpu.roll(value, 1, axis)

    def diff(value, axis):
        return nxt(value, axis) - prv(value, axis)

    def forward(start, count, c, masked):
        h, u, v = (wide(S, (f,), start, count, c) for f in range(3))
        d = wide(D, (), start, count, c)
        if masked:
            index = (
                tile * rows - PAD + start + lax.broadcasted_iota(jnp.int32, h.shape, 0)
            )
            inside = (index >= 0) & (index < tiles * rows)
        for _ in range(FSTEPS):
            new_h = h - (time_step * 0.5) * (diff(d * u, 0) + diff(d * v, 1))
            if masked:
                new_h = jnp.where(inside, new_h, 0.0)
            new_u = u - (time_step * gravity * 0.5) * diff(new_h, 0) + (time_step * coriolis) * v
            new_v = v - (time_step * gravity * 0.5) * diff(new_h, 1) - (time_step * coriolis) * u
            h, u, v = new_h, new_u, new_v
        return h, u, v

    later = jnp.minimum(me + 1, subs - 1)
    keep = jnp.where(me < subs - 1, 1.0, 0.0)

    def weights(s):
        return mixing[s, me], mixing[s, later] * keep

    dest_pair = [lax.rem(pair + k, pairs) for k in range(pairs)]
    w_mine = [weights(q * 2 + parity) for q in dest_pair]
    w_mate = [weights(q * 2 + 1 - parity) for q in dest_pair]

    edge = PAD
    inner = rows - 2 * edge
    blocks = {
        "inner": (edge, inner),
        "top": (0, edge),
        "bottom": (rows - edge, edge),
    }
    numbers = {"inner": 0, "top": 1, "bottom": 2}

    def a_copy(name, c, k):
        row, count = blocks[name]
        at = (k, slice(None), pl.ds(row, count), pl.ds(c * CHUNK, CHUNK))
        return pltpu.make_async_remote_copy(
            src_ref=send_a.at[at], dst_ref=recv_a.at[at],
            send_sem=a_send.at[k, numbers[name], c], recv_sem=a_recv.at[k, numbers[name], c],
            device_id={"sub": mate}, device_id_type=pl.DeviceIdType.MESH,
        )

    def b_copy(name, c, k):
        row, count = blocks[name]
        at = (k - 1, slice(None), pl.ds(row, count), pl.ds(c * CHUNK, CHUNK))
        return pltpu.make_async_remote_copy(
            src_ref=send_b.at[at], dst_ref=recv_b.at[at],
            send_sem=b_send.at[k - 1, numbers[name], c],
            recv_sem=b_recv.at[k - 1, numbers[name], c],
            device_id={"sub": dest_pair[k] * 2 + parity},
            device_id_type=pl.DeviceIdType.MESH,
        )

    def terms(name, c):
        row, count = blocks[name]
        if name == "inner":
            ends = forward(PAD, rows, c, False)
            skip = edge
        else:
            ends = forward(row, PAD + edge + PAD, c, True)
            skip = PAD
        span = pl.ds(c * CHUNK, CHUNK)
        order = list(range(1, pairs)) + [0]
        for k in order:
            for f in range(3):
                end = ends[f][skip:skip + count, LANES:LANES + CHUNK]
                start = S[f, pl.ds(PAD + row, count), span]
                a, b = w_mate[k]
                send_a[k, f, pl.ds(row, count), span] = a * start - b * end
                a, b = w_mine[k]
                mine = a * start - b * end
                if k == 0:
                    M[f, pl.ds(PAD + row, count), span] = mine
                else:
                    send_b[k - 1, f, pl.ds(row, count), span] = mine
            a_copy(name, c, k).start()

    def join(name, c):
        row, count = blocks[name]
        span = pl.ds(c * CHUNK, CHUNK)
        for k in list(range(1, pairs)) + [0]:
            a_copy(name, c, k).wait_recv()
            for f in range(3):
                got = recv_a[k, f, pl.ds(row, count), span]
                if k == 0:
                    at = (f, pl.ds(PAD + row, count), span)
                    M[at] = M[at] + got
                else:
                    at = (k - 1, f, pl.ds(row, count), span)
                    send_b[at] = send_b[at] + got
            if k > 0:
                b_copy(name, c, k).start()

    def finish(name, c):
        row, count = blocks[name]
        span = pl.ds(c * CHUNK, CHUNK)
        for k in range(1, pairs):
            b_copy(name, c, k).wait_recv()
        for f in range(3):
            at = (f, pl.ds(PAD + row, count), span)
            total = M[at]
            for k in range(1, pairs):
                total = total + recv_b[k - 1, f, pl.ds(row, count), span]
            M[at] = total

    def m_copy(way, c):
        span = pl.ds(c * CHUNK, CHUNK)
        if way == 0:
            source, target, where = pl.ds(PAD + rows - DSTEPS, DSTEPS), pl.ds(PAD - DSTEPS, DSTEPS), down
        else:
            source, target, where = pl.ds(PAD, DSTEPS), pl.ds(PAD + rows, DSTEPS), up
        return pltpu.make_async_remote_copy(
            src_ref=M.at[:, source, span], dst_ref=M.at[:, target, span],
            send_sem=m_send.at[way, c], recv_sem=m_recv.at[way, c],
            device_id={"tile": where}, device_id_type=pl.DeviceIdType.MESH,
        )

    def send_mixed(c):
        @pl.when(has_down)
        def _():
            m_copy(0, c).start()

        @pl.when(has_up)
        def _():
            m_copy(1, c).start()

    def take_mixed(c):
        @pl.when(has_up)
        def _():
            m_copy(0, c).wait_recv()

        @pl.when(has_down)
        def _():
            m_copy(1, c).wait_recv()

    def diffuse(c):
        total = rows + 2 * PAD
        kappa = wide(K, (), 0, total, c)
        for f in range(3):
            w = wide(M, (f,), 0, total, c)
            for _ in range(DSTEPS):
                near = nxt(w, 0) + prv(w, 0) + nxt(w, 1) + prv(w, 1)
                w = w + kappa * (near - 4.0 * w)
            out[0, f, :, pl.ds(c * CHUNK, CHUNK)] = w[PAD:PAD + rows, LANES:LANES + CHUNK]

    terms("inner", 0)
    for c in range(1, nch):
        terms("inner", c)
        join("inner", c - 1)
    join("inner", nch - 1)

    @pl.when(has_up)
    def _():
        for copy in to_down:
            copy.wait_recv()

    @pl.when(has_down)
    def _():
        for copy in to_up:
            copy.wait_recv()

    lookup(0, PAD)
    lookup(PAD + rows, PAD)

    def edge_terms(c):
        terms("top", c)
        terms("bottom", c)

    def edge_join(c):
        join("top", c)
        join("bottom", c)

    edge_terms(0)
    for c in range(1, nch):
        edge_terms(c)
        edge_join(c - 1)
    edge_join(nch - 1)
    for c in range(nch):
        finish("inner", c)
    done = []
    for c in range(nch):
        finish("top", c)
        finish("bottom", c)
        send_mixed(c)
        if c >= 2:
            if c == 2:
                take_mixed(0)
                take_mixed(1)
            take_mixed(c)
            if c < nch - 1 or nch == 3:
                diffuse(c - 1)
                done.append(c - 1)
    if nch <= 2:
        for c in range(nch):
            take_mixed(c)
    for c in range(nch):
        if c not in done:
            diffuse(c)

    for c in range(nch):
        for name in blocks:
            for k in range(pairs):
                a_copy(name, c, k).wait_send()
                if k > 0:
                    b_copy(name, c, k).wait_send()

    @pl.when(has_down)
    def _():
        for copy in to_down:
            copy.wait_send()
        for c in range(nch):
            m_copy(0, c).wait_send()

    @pl.when(has_up)
    def _():
        for copy in to_up:
            copy.wait_send()
        for c in range(nch):
            m_copy(1, c).wait_send()


def solution(mesh):
    subs, tiles = mesh.shape["sub"], mesh.shape["tile"]

    def local(states, terrain, depth_table, spread_table, mixing):
        _, fields, rows, cols = states.shape
        pairs = subs // 2
        nch = cols // CHUNK
        tall = rows + 2 * PAD
        dma = pltpu.SemaphoreType.DMA
        many = max(pairs - 1, 1)
        return pl.pallas_call(
            functools.partial(kernel, subs, tiles, rows, cols, depth_table.shape[0]),
            out_shape=jax.ShapeDtypeStruct(states.shape, jnp.float32),
            in_specs=[pl.BlockSpec(memory_space=pl.ANY)] * 2
            + [pl.BlockSpec(memory_space=pltpu.SMEM)] * 3,
            out_specs=pl.BlockSpec(memory_space=pltpu.VMEM),
            scratch_shapes=[
                pltpu.VMEM((fields, tall, cols), jnp.float32),
                pltpu.VMEM((tall, cols), jnp.int32),
                pltpu.VMEM((tall, cols), jnp.float32),
                pltpu.VMEM((tall, cols), jnp.float32),
                pltpu.VMEM((pairs, fields, rows, cols), jnp.float32),
                pltpu.VMEM((pairs, fields, rows, cols), jnp.float32),
                pltpu.VMEM((many, fields, rows, cols), jnp.float32),
                pltpu.VMEM((many, fields, rows, cols), jnp.float32),
                pltpu.VMEM((fields, tall, cols), jnp.float32),
                dma((2,)),
                dma((4,)),
                dma((4,)),
                dma((pairs, 3, nch)),
                dma((pairs, 3, nch)),
                dma((many, 3, nch)),
                dma((many, 3, nch)),
                dma((2, nch)),
                dma((2, nch)),
            ],
            compiler_params=pltpu.CompilerParams(
                collective_id=0, has_side_effects=True, vmem_limit_bytes=48 * 1024 * 1024
            ),
            name="gradient",
        )(states, terrain, depth_table, spread_table, mixing)

    in_specs = (P("sub", None, "tile", None), P("tile", None), P(), P(), P())
    out_specs = P("sub", None, "tile", None)
    return jax.shard_map(local, mesh=mesh, in_specs=in_specs, out_specs=out_specs, check_vma=False)
```

```python
import functools

import jax
import jax.numpy as jnp
from jax import lax
from jax.experimental import pallas as pl
from jax.experimental.pallas import tpu as pltpu
from jax.sharding import PartitionSpec as P

FSTEPS = 3
DSTEPS = 3
time_step = 0.5
gravity = 1.0
coriolis = 0.3

PAD = 8
LANES = 128
FHALO = 2 * FSTEPS
CHUNK = 512


def kernel(
    subs, tiles, rows, cols, nclass,
    states, terrain, depth_in, spread_in, mixing_in, out,
    depth_tab, spread_tab, mixing, S, T, D, K, send_a, recv_a, send_b, recv_b, M,
    load_sem, halo_send, halo_recv, a_send, a_recv, b_send, b_recv, m_send, m_recv,
):
    pairs = subs // 2
    nch = cols // CHUNK
    me = lax.axis_index("sub")
    tile = lax.axis_index("tile")
    parity = lax.rem(me, 2)
    mate = me + 1 - 2 * parity
    pair = me // 2
    has_up = tile > 0
    has_down = tile < tiles - 1
    up, down = tile - 1, tile + 1

    loads = [
        pltpu.make_async_copy(states.at[0], S.at[:, pl.ds(PAD, rows), :], load_sem.at[0]),
        pltpu.make_async_copy(terrain, T.at[pl.ds(PAD, rows), :], load_sem.at[1]),
        pltpu.make_async_copy(depth_in, depth_tab, load_sem.at[2]),
        pltpu.make_async_copy(spread_in, spread_tab, load_sem.at[3]),
        pltpu.make_async_copy(mixing_in, mixing, load_sem.at[4]),
    ]
    for copy in loads:
        copy.start()

    barrier = pltpu.get_barrier_semaphore()
    pl.semaphore_signal(barrier, inc=1, device_id={"sub": mate})
    for k in range(1, pairs):
        pl.semaphore_signal(
            barrier, inc=1, device_id={"sub": lax.rem(pair + k, pairs) * 2 + parity}
        )

    @pl.when(has_up)
    def _():
        pl.semaphore_signal(barrier, inc=1, device_id={"tile": up})

    @pl.when(has_down)
    def _():
        pl.semaphore_signal(barrier, inc=1, device_id={"tile": down})

    pl.semaphore_wait(
        barrier, pairs + has_up.astype(jnp.int32) + has_down.astype(jnp.int32)
    )

    def halo_copy(source, target, index, where):
        return pltpu.make_async_remote_copy(
            src_ref=source, dst_ref=target, send_sem=halo_send.at[index[0], index[1]],
            recv_sem=halo_recv.at[index[0], index[1]], device_id={"tile": where},
            device_id_type=pl.DeviceIdType.MESH,
        )

    last, first = pl.ds(rows - FHALO, FHALO), pl.ds(0, FHALO)
    above, below = pl.ds(PAD - FHALO, FHALO), pl.ds(PAD + rows, FHALO)
    spans = [(cols - LANES, LANES)]
    for c in range(nch):
        begin = c * CHUNK + LANES if c > 0 else 0
        spans.append((begin, min((c + 1) * CHUNK + LANES, cols - LANES) - begin))

    def to_down(piece):
        at = pl.ds(*spans[piece])
        return [
            halo_copy(terrain.at[last, at], T.at[above, at], (0, piece), down),
            halo_copy(states.at[0, :, last, at], S.at[:, above, at], (1, piece), down),
        ]

    def to_up(piece):
        at = pl.ds(*spans[piece])
        return [
            halo_copy(terrain.at[first, at], T.at[below, at], (2, piece), up),
            halo_copy(states.at[0, :, first, at], S.at[:, below, at], (3, piece), up),
        ]

    for piece in range(nch + 1):

        @pl.when(has_down)
        def _():
            for copy in to_down(piece):
                copy.start()

        @pl.when(has_up)
        def _():
            for copy in to_up(piece):
                copy.start()

    S[:, 0:PAD - FHALO, :] = jnp.zeros((3, PAD - FHALO, cols), jnp.float32)
    T[0:PAD - FHALO, :] = jnp.full((PAD - FHALO, cols), -1, jnp.int32)
    S[:, PAD + rows + FHALO:, :] = jnp.zeros((3, PAD - FHALO, cols), jnp.float32)
    T[PAD + rows + FHALO:, :] = jnp.full((PAD - FHALO, cols), -1, jnp.int32)
    M[:, 0:PAD - DSTEPS, :] = jnp.zeros((3, PAD - DSTEPS, cols), jnp.float32)
    M[:, PAD + rows + DSTEPS:, :] = jnp.zeros((3, PAD - DSTEPS, cols), jnp.float32)

    @pl.when(jnp.logical_not(has_up))
    def _():
        S[:, PAD - FHALO:PAD, :] = jnp.zeros((3, FHALO, cols), jnp.float32)
        T[PAD - FHALO:PAD, :] = jnp.full((FHALO, cols), -1, jnp.int32)
        M[:, PAD - DSTEPS:PAD, :] = jnp.zeros((3, DSTEPS, cols), jnp.float32)

    @pl.when(jnp.logical_not(has_down))
    def _():
        S[:, PAD + rows:PAD + rows + FHALO, :] = jnp.zeros((3, FHALO, cols), jnp.float32)
        T[PAD + rows:PAD + rows + FHALO, :] = jnp.full((FHALO, cols), -1, jnp.int32)
        M[:, PAD + rows:PAD + rows + DSTEPS, :] = jnp.zeros((3, DSTEPS, cols), jnp.float32)

    def lookup(start, count, begin, width):
        at = (pl.ds(start, count), pl.ds(begin, width))
        kind = T[at]
        depth = jnp.zeros(kind.shape, jnp.float32)
        kappa = jnp.zeros(kind.shape, jnp.float32)
        for n in range(nclass):
            hit = kind == n
            depth = jnp.where(hit, depth_tab[n], depth)
            kappa = jnp.where(hit, spread_tab[n], kappa)
        D[at] = depth
        K[at] = kappa

    def take_halo(piece):
        @pl.when(has_up)
        def _():
            for copy in to_down(piece):
                copy.wait_recv()

        @pl.when(has_down)
        def _():
            for copy in to_up(piece):
                copy.wait_recv()

        lookup(0, PAD, *spans[piece])
        lookup(PAD + rows, PAD, *spans[piece])

    for copy in loads:
        copy.wait()
    for c in range(nch):
        lookup(PAD, rows, c * CHUNK, CHUNK)

    def wide(ref, lead, start, count, begin):
        begin, width = (begin - LANES) % cols, CHUNK + 2 * LANES
        parts = []
        while width > 0:
            size = min(width, cols - begin)
            parts.append(ref[lead + (pl.ds(start, count), pl.ds(begin, size))])
            begin, width = (begin + size) % cols, width - size
        return parts[0] if len(parts) == 1 else jnp.concatenate(parts, axis=-1)

    def nxt(value, axis):
        return pltpu.roll(value, value.shape[axis] - 1, axis)

    def prv(value, axis):
        return pltpu.roll(value, 1, axis)

    def diff(value, axis):
        return nxt(value, axis) - prv(value, axis)

    def forward(start, count, c, masked):
        h, u, v = (wide(S, (f,), start, count, c * CHUNK) for f in range(3))
        d = wide(D, (), start, count, c * CHUNK)
        if masked:
            index = (
                tile * rows - PAD + start + lax.broadcasted_iota(jnp.int32, h.shape, 0)
            )
            inside = (index >= 0) & (index < tiles * rows)
        for _ in range(FSTEPS):
            new_h = h - (time_step * 0.5) * (diff(d * u, 0) + diff(d * v, 1))
            if masked:
                new_h = jnp.where(inside, new_h, 0.0)
            new_u = u - (time_step * gravity * 0.5) * diff(new_h, 0) + (time_step * coriolis) * v
            new_v = v - (time_step * gravity * 0.5) * diff(new_h, 1) - (time_step * coriolis) * u
            h, u, v = new_h, new_u, new_v
        return h, u, v

    later = jnp.minimum(me + 1, subs - 1)
    keep = jnp.where(me < subs - 1, 1.0, 0.0)

    def weights(s):
        return mixing[s, me], mixing[s, later] * keep

    dest_pair = [lax.rem(pair + k, pairs) for k in range(pairs)]
    w_mine = [weights(q * 2 + parity) for q in dest_pair]
    w_mate = [weights(q * 2 + 1 - parity) for q in dest_pair]

    edge = PAD
    inner = rows - 2 * edge
    blocks = {
        "inner": (edge, inner),
        "top": (0, edge),
        "bottom": (rows - edge, edge),
    }
    numbers = {"inner": 0, "top": 1, "bottom": 2}

    def a_copy(name, c, k):
        row, count = blocks[name]
        at = (k, slice(None), pl.ds(row, count), pl.ds(c * CHUNK, CHUNK))
        return pltpu.make_async_remote_copy(
            src_ref=send_a.at[at], dst_ref=recv_a.at[at],
            send_sem=a_send.at[k, numbers[name], c], recv_sem=a_recv.at[k, numbers[name], c],
            device_id={"sub": mate}, device_id_type=pl.DeviceIdType.MESH,
        )

    def b_copy(name, c, k):
        row, count = blocks[name]
        at = (k - 1, slice(None), pl.ds(row, count), pl.ds(c * CHUNK, CHUNK))
        return pltpu.make_async_remote_copy(
            src_ref=send_b.at[at], dst_ref=recv_b.at[at],
            send_sem=b_send.at[k - 1, numbers[name], c],
            recv_sem=b_recv.at[k - 1, numbers[name], c],
            device_id={"sub": dest_pair[k] * 2 + parity},
            device_id_type=pl.DeviceIdType.MESH,
        )

    def terms(name, c):
        row, count = blocks[name]
        if name == "inner":
            ends = forward(PAD, rows, c, False)
            skip = edge
        else:
            ends = forward(row, PAD + edge + PAD, c, True)
            skip = PAD
        span = pl.ds(c * CHUNK, CHUNK)
        order = list(range(1, pairs)) + [0]
        for k in order:
            for f in range(3):
                end = ends[f][skip:skip + count, LANES:LANES + CHUNK]
                start = S[f, pl.ds(PAD + row, count), span]
                a, b = w_mate[k]
                send_a[k, f, pl.ds(row, count), span] = a * start - b * end
                a, b = w_mine[k]
                mine = a * start - b * end
                if k == 0:
                    M[f, pl.ds(PAD + row, count), span] = mine
                else:
                    send_b[k - 1, f, pl.ds(row, count), span] = mine
            a_copy(name, c, k).start()

    def join(name, c):
        row, count = blocks[name]
        span = pl.ds(c * CHUNK, CHUNK)
        for k in list(range(1, pairs)) + [0]:
            a_copy(name, c, k).wait_recv()
            for f in range(3):
                got = recv_a[k, f, pl.ds(row, count), span]
                if k == 0:
                    at = (f, pl.ds(PAD + row, count), span)
                    M[at] = M[at] + got
                else:
                    at = (k - 1, f, pl.ds(row, count), span)
                    send_b[at] = send_b[at] + got
            if k > 0:
                b_copy(name, c, k).start()

    def finish(name, c):
        row, count = blocks[name]
        span = pl.ds(c * CHUNK, CHUNK)
        for k in range(1, pairs):
            b_copy(name, c, k).wait_recv()
        for f in range(3):
            at = (f, pl.ds(PAD + row, count), span)
            total = M[at]
            for k in range(1, pairs):
                total = total + recv_b[k - 1, f, pl.ds(row, count), span]
            M[at] = total

    def m_copy(way, c):
        span = pl.ds(c * CHUNK, CHUNK)
        if way == 0:
            source, target, where = pl.ds(PAD + rows - DSTEPS, DSTEPS), pl.ds(PAD - DSTEPS, DSTEPS), down
        else:
            source, target, where = pl.ds(PAD, DSTEPS), pl.ds(PAD + rows, DSTEPS), up
        return pltpu.make_async_remote_copy(
            src_ref=M.at[:, source, span], dst_ref=M.at[:, target, span],
            send_sem=m_send.at[way, c], recv_sem=m_recv.at[way, c],
            device_id={"tile": where}, device_id_type=pl.DeviceIdType.MESH,
        )

    def send_mixed(c):
        @pl.when(has_down)
        def _():
            m_copy(0, c).start()

        @pl.when(has_up)
        def _():
            m_copy(1, c).start()

    def take_mixed(c):
        @pl.when(has_up)
        def _():
            m_copy(0, c).wait_recv()

        @pl.when(has_down)
        def _():
            m_copy(1, c).wait_recv()

    def diffuse(c):
        begin = c * CHUNK - LANES
        total = rows + 2 * PAD
        kappa = wide(K, (), 0, total, begin)
        for f in range(3):
            w = wide(M, (f,), 0, total, begin)
            for _ in range(DSTEPS):
                near = nxt(w, 0) + prv(w, 0) + nxt(w, 1) + prv(w, 1)
                w = w + kappa * (near - 4.0 * w)
            w = w[PAD:PAD + rows, LANES:LANES + CHUNK]
            if c > 0:
                out[0, f, :, pl.ds(begin, CHUNK)] = w
            else:
                out[0, f, :, pl.ds(cols - LANES, LANES)] = w[:, :LANES]
                out[0, f, :, pl.ds(0, CHUNK - LANES)] = w[:, LANES:]

    def edge_terms(c):
        take_halo(c + 1)
        terms("top", c)
        terms("bottom", c)

    def edge_join(c):
        join("top", c)
        join("bottom", c)

    terms("inner", 0)
    for c in range(1, nch):
        terms("inner", c)
        join("inner", c - 1)
    take_halo(0)
    edge_terms(0)
    join("inner", nch - 1)
    for c in range(1, nch):
        edge_terms(c)
        edge_join(c - 1)
    edge_join(nch - 1)
    for c in range(nch):
        finish("inner", c)
    for c in range(nch):
        finish("top", c)
        finish("bottom", c)
        send_mixed(c)
        if c >= 2:
            take_mixed(c - 1)
            if c == 2:
                take_mixed(0)
            diffuse(c - 1)
    take_mixed(nch - 1)
    if nch == 2:
        take_mixed(0)
    diffuse(nch - 1)
    diffuse(0)

    for c in range(nch):
        for name in blocks:
            for k in range(pairs):
                a_copy(name, c, k).wait_send()
                if k > 0:
                    b_copy(name, c, k).wait_send()

    @pl.when(has_down)
    def _():
        for piece in range(nch + 1):
            for copy in to_down(piece):
                copy.wait_send()
        for c in range(nch):
            m_copy(0, c).wait_send()

    @pl.when(has_up)
    def _():
        for piece in range(nch + 1):
            for copy in to_up(piece):
                copy.wait_send()
        for c in range(nch):
            m_copy(1, c).wait_send()


def solution(mesh):
    subs, tiles = mesh.shape["sub"], mesh.shape["tile"]

    def local(states, terrain, depth_table, spread_table, mixing):
        _, fields, rows, cols = states.shape
        pairs = subs // 2
        nch = cols // CHUNK
        tall = rows + 2 * PAD
        dma = pltpu.SemaphoreType.DMA
        many = max(pairs - 1, 1)
        return pl.pallas_call(
            functools.partial(kernel, subs, tiles, rows, cols, depth_table.shape[0]),
            out_shape=jax.ShapeDtypeStruct(states.shape, jnp.float32),
            in_specs=[pl.BlockSpec(memory_space=pltpu.HBM)] * 5,
            out_specs=pl.BlockSpec(memory_space=pltpu.VMEM),
            scratch_shapes=[
                pltpu.SMEM(depth_table.shape, jnp.float32),
                pltpu.SMEM(spread_table.shape, jnp.float32),
                pltpu.SMEM(mixing.shape, jnp.float32),
                pltpu.VMEM((fields, tall, cols), jnp.float32),
                pltpu.VMEM((tall, cols), jnp.int32),
                pltpu.VMEM((tall, cols), jnp.float32),
                pltpu.VMEM((tall, cols), jnp.float32),
                pltpu.VMEM((pairs, fields, rows, cols), jnp.float32),
                pltpu.VMEM((pairs, fields, rows, cols), jnp.float32),
                pltpu.VMEM((many, fields, rows, cols), jnp.float32),
                pltpu.VMEM((many, fields, rows, cols), jnp.float32),
                pltpu.VMEM((fields, tall, cols), jnp.float32),
                dma((5,)),
                dma((4, nch + 1)),
                dma((4, nch + 1)),
                dma((pairs, 3, nch)),
                dma((pairs, 3, nch)),
                dma((many, 3, nch)),
                dma((many, 3, nch)),
                dma((2, nch)),
                dma((2, nch)),
            ],
            compiler_params=pltpu.CompilerParams(
                collective_id=0, has_side_effects=True, vmem_limit_bytes=67043328
            ),
            name="gradient",
        )(states, terrain, depth_table, spread_table, mixing)

    in_specs = (P("sub", None, "tile", None), P("tile", None), P(), P(), P())
    out_specs = P("sub", None, "tile", None)
    return jax.shard_map(local, mesh=mesh, in_specs=in_specs, out_specs=out_specs, check_vma=False)
```

```python
import functools

import jax
import jax.numpy as jnp
from jax import lax
from jax.experimental import pallas as pl
from jax.experimental.pallas import tpu as pltpu
from jax.sharding import PartitionSpec as P

FSTEPS = 3
DSTEPS = 3
time_step = 0.5
gravity = 1.0
coriolis = 0.3

PAD = 8
LANES = 128
FHALO = 2 * FSTEPS
CHUNK = 512


def kernel(
    subs, tiles, rows, cols, nclass,
    states, terrain, depth_in, spread_in, mixing_in, out,
    depth_tab, spread_tab, mixing, S, T, D, K, send_a, recv_a, send_b, recv_b, M,
    load_sem, halo_send, halo_recv, a_send, a_recv, b_send, b_recv, m_send, m_recv,
):
    pairs = subs // 2
    nch = cols // CHUNK
    me = lax.axis_index("sub")
    tile = lax.axis_index("tile")
    parity = lax.rem(me, 2)
    mate = me + 1 - 2 * parity
    pair = me // 2
    has_up = tile > 0
    has_down = tile < tiles - 1
    up, down = tile - 1, tile + 1

    loads = [
        pltpu.make_async_copy(states.at[0], S.at[:, pl.ds(PAD, rows), :], load_sem.at[0]),
        pltpu.make_async_copy(terrain, T.at[pl.ds(PAD, rows), :], load_sem.at[1]),
        pltpu.make_async_copy(depth_in, depth_tab, load_sem.at[2]),
        pltpu.make_async_copy(spread_in, spread_tab, load_sem.at[3]),
        pltpu.make_async_copy(mixing_in, mixing, load_sem.at[4]),
    ]
    for copy in loads:
        copy.start()

    barrier = pltpu.get_barrier_semaphore()
    pl.semaphore_signal(barrier, inc=1, device_id={"sub": mate})
    for k in range(1, pairs):
        pl.semaphore_signal(
            barrier, inc=1, device_id={"sub": lax.rem(pair + k, pairs) * 2 + parity}
        )

    @pl.when(has_up)
    def _():
        pl.semaphore_signal(barrier, inc=1, device_id={"tile": up})

    @pl.when(has_down)
    def _():
        pl.semaphore_signal(barrier, inc=1, device_id={"tile": down})

    pl.semaphore_wait(
        barrier, pairs + has_up.astype(jnp.int32) + has_down.astype(jnp.int32)
    )

    def halo_copy(source, target, index, where):
        return pltpu.make_async_remote_copy(
            src_ref=source, dst_ref=target, send_sem=halo_send.at[index[0], index[1]],
            recv_sem=halo_recv.at[index[0], index[1]], device_id={"tile": where},
            device_id_type=pl.DeviceIdType.MESH,
        )

    last, first = pl.ds(rows - FHALO, FHALO), pl.ds(0, FHALO)
    above, below = pl.ds(PAD - FHALO, FHALO), pl.ds(PAD + rows, FHALO)
    spans = [(cols - LANES, LANES)]
    for c in range(nch):
        begin = c * CHUNK + LANES if c > 0 else 0
        spans.append((begin, min((c + 1) * CHUNK + LANES, cols - LANES) - begin))

    def to_down(piece):
        at = pl.ds(*spans[piece])
        return [
            halo_copy(terrain.at[last, at], T.at[above, at], (0, piece), down),
            halo_copy(states.at[0, :, last, at], S.at[:, above, at], (1, piece), down),
        ]

    def to_up(piece):
        at = pl.ds(*spans[piece])
        return [
            halo_copy(terrain.at[first, at], T.at[below, at], (2, piece), up),
            halo_copy(states.at[0, :, first, at], S.at[:, below, at], (3, piece), up),
        ]

    for piece in range(nch + 1):

        @pl.when(has_down)
        def _():
            for copy in to_down(piece):
                copy.start()

        @pl.when(has_up)
        def _():
            for copy in to_up(piece):
                copy.start()

    S[:, 0:PAD - FHALO, :] = jnp.zeros((3, PAD - FHALO, cols), jnp.float32)
    T[0:PAD - FHALO, :] = jnp.full((PAD - FHALO, cols), -1, jnp.int32)
    S[:, PAD + rows + FHALO:, :] = jnp.zeros((3, PAD - FHALO, cols), jnp.float32)
    T[PAD + rows + FHALO:, :] = jnp.full((PAD - FHALO, cols), -1, jnp.int32)
    M[:, 0:PAD - DSTEPS, :] = jnp.zeros((3, PAD - DSTEPS, cols), jnp.float32)
    M[:, PAD + rows + DSTEPS:, :] = jnp.zeros((3, PAD - DSTEPS, cols), jnp.float32)

    @pl.when(jnp.logical_not(has_up))
    def _():
        S[:, PAD - FHALO:PAD, :] = jnp.zeros((3, FHALO, cols), jnp.float32)
        T[PAD - FHALO:PAD, :] = jnp.full((FHALO, cols), -1, jnp.int32)
        M[:, PAD - DSTEPS:PAD, :] = jnp.zeros((3, DSTEPS, cols), jnp.float32)

    @pl.when(jnp.logical_not(has_down))
    def _():
        S[:, PAD + rows:PAD + rows + FHALO, :] = jnp.zeros((3, FHALO, cols), jnp.float32)
        T[PAD + rows:PAD + rows + FHALO, :] = jnp.full((FHALO, cols), -1, jnp.int32)
        M[:, PAD + rows:PAD + rows + DSTEPS, :] = jnp.zeros((3, DSTEPS, cols), jnp.float32)

    def lookup(start, count, begin, width):
        at = (pl.ds(start, count), pl.ds(begin, width))
        kind = T[at]
        depth = jnp.zeros(kind.shape, jnp.float32)
        kappa = jnp.zeros(kind.shape, jnp.float32)
        for n in range(nclass):
            hit = kind == n
            depth = jnp.where(hit, depth_tab[n], depth)
            kappa = jnp.where(hit, spread_tab[n], kappa)
        D[at] = depth
        K[at] = kappa

    def take_halo(piece):
        @pl.when(has_up)
        def _():
            for copy in to_down(piece):
                copy.wait_recv()

        @pl.when(has_down)
        def _():
            for copy in to_up(piece):
                copy.wait_recv()

        lookup(0, PAD, *spans[piece])
        lookup(PAD + rows, PAD, *spans[piece])

    for copy in loads:
        copy.wait()
    for c in range(nch):
        lookup(PAD, rows, c * CHUNK, CHUNK)

    def wide(ref, lead, start, count, begin):
        begin, width = (begin - LANES) % cols, CHUNK + 2 * LANES
        parts = []
        while width > 0:
            size = min(width, cols - begin)
            parts.append(ref[lead + (pl.ds(start, count), pl.ds(begin, size))])
            begin, width = (begin + size) % cols, width - size
        return parts[0] if len(parts) == 1 else jnp.concatenate(parts, axis=-1)

    def nxt(value, axis):
        return pltpu.roll(value, value.shape[axis] - 1, axis)

    def prv(value, axis):
        return pltpu.roll(value, 1, axis)

    def diff(value, axis):
        return nxt(value, axis) - prv(value, axis)

    def forward(start, count, c, masked):
        h, u, v = (wide(S, (f,), start, count, c * CHUNK) for f in range(3))
        d = wide(D, (), start, count, c * CHUNK)
        if masked:
            index = (
                tile * rows - PAD + start + lax.broadcasted_iota(jnp.int32, h.shape, 0)
            )
            inside = (index >= 0) & (index < tiles * rows)
        for _ in range(FSTEPS):
            new_h = h - (time_step * 0.5) * (diff(d * u, 0) + diff(d * v, 1))
            if masked:
                new_h = jnp.where(inside, new_h, 0.0)
            new_u = u - (time_step * gravity * 0.5) * diff(new_h, 0) + (time_step * coriolis) * v
            new_v = v - (time_step * gravity * 0.5) * diff(new_h, 1) - (time_step * coriolis) * u
            h, u, v = new_h, new_u, new_v
        return h, u, v

    later = jnp.minimum(me + 1, subs - 1)
    keep = jnp.where(me < subs - 1, 1.0, 0.0)

    def weights(s):
        return mixing[s, me], mixing[s, later] * keep

    dest_pair = [lax.rem(pair + k, pairs) for k in range(pairs)]
    w_mine = [weights(q * 2 + parity) for q in dest_pair]
    w_mate = [weights(q * 2 + 1 - parity) for q in dest_pair]

    edge = PAD
    inner = rows - 2 * edge
    blocks = {
        "inner": (edge, inner),
        "top": (0, edge),
        "bottom": (rows - edge, edge),
    }
    numbers = {"inner": 0, "top": 1, "bottom": 2}

    def a_copy(name, c, k):
        row, count = blocks[name]
        at = (k, slice(None), pl.ds(row, count), pl.ds(c * CHUNK, CHUNK))
        return pltpu.make_async_remote_copy(
            src_ref=send_a.at[at], dst_ref=recv_a.at[at],
            send_sem=a_send.at[k, numbers[name], c], recv_sem=a_recv.at[k, numbers[name], c],
            device_id={"sub": mate}, device_id_type=pl.DeviceIdType.MESH,
        )

    def b_copy(name, c, k):
        row, count = blocks[name]
        at = (k - 1, slice(None), pl.ds(row, count), pl.ds(c * CHUNK, CHUNK))
        return pltpu.make_async_remote_copy(
            src_ref=send_b.at[at], dst_ref=recv_b.at[at],
            send_sem=b_send.at[k - 1, numbers[name], c],
            recv_sem=b_recv.at[k - 1, numbers[name], c],
            device_id={"sub": dest_pair[k] * 2 + parity},
            device_id_type=pl.DeviceIdType.MESH,
        )

    def terms(name, c):
        row, count = blocks[name]
        if name == "inner":
            ends = forward(PAD, rows, c, False)
            skip = edge
        else:
            ends = forward(row, PAD + edge + PAD, c, True)
            skip = PAD
        span = pl.ds(c * CHUNK, CHUNK)
        order = list(range(1, pairs)) + [0]
        for k in order:
            for f in range(3):
                end = ends[f][skip:skip + count, LANES:LANES + CHUNK]
                start = S[f, pl.ds(PAD + row, count), span]
                a, b = w_mate[k]
                send_a[k, f, pl.ds(row, count), span] = a * start - b * end
                a, b = w_mine[k]
                mine = a * start - b * end
                if k == 0:
                    M[f, pl.ds(PAD + row, count), span] = mine
                else:
                    send_b[k - 1, f, pl.ds(row, count), span] = mine
            a_copy(name, c, k).start()

    def join(name, c):
        row, count = blocks[name]
        span = pl.ds(c * CHUNK, CHUNK)
        for k in list(range(1, pairs)) + [0]:
            a_copy(name, c, k).wait_recv()
            for f in range(3):
                got = recv_a[k, f, pl.ds(row, count), span]
                if k == 0:
                    at = (f, pl.ds(PAD + row, count), span)
                    M[at] = M[at] + got
                else:
                    at = (k - 1, f, pl.ds(row, count), span)
                    send_b[at] = send_b[at] + got
            if k > 0:
                b_copy(name, c, k).start()

    def finish(name, c):
        row, count = blocks[name]
        span = pl.ds(c * CHUNK, CHUNK)
        for k in range(1, pairs):
            b_copy(name, c, k).wait_recv()
        for f in range(3):
            at = (f, pl.ds(PAD + row, count), span)
            total = M[at]
            for k in range(1, pairs):
                total = total + recv_b[k - 1, f, pl.ds(row, count), span]
            M[at] = total

    def m_copy(way, c):
        span = pl.ds(c * CHUNK, CHUNK)
        if way == 0:
            source, target, where = pl.ds(PAD + rows - DSTEPS, DSTEPS), pl.ds(PAD - DSTEPS, DSTEPS), down
        else:
            source, target, where = pl.ds(PAD, DSTEPS), pl.ds(PAD + rows, DSTEPS), up
        return pltpu.make_async_remote_copy(
            src_ref=M.at[:, source, span], dst_ref=M.at[:, target, span],
            send_sem=m_send.at[way, c], recv_sem=m_recv.at[way, c],
            device_id={"tile": where}, device_id_type=pl.DeviceIdType.MESH,
        )

    def send_mixed(c):
        @pl.when(has_down)
        def _():
            m_copy(0, c).start()

        @pl.when(has_up)
        def _():
            m_copy(1, c).start()

    def take_mixed(c):
        @pl.when(has_up)
        def _():
            m_copy(0, c).wait_recv()

        @pl.when(has_down)
        def _():
            m_copy(1, c).wait_recv()

    def diffuse(c):
        begin = c * CHUNK - LANES
        total = rows + 2 * PAD
        kappa = wide(K, (), 0, total, begin)
        for f in range(3):
            w = wide(M, (f,), 0, total, begin)
            for _ in range(DSTEPS):
                near = nxt(w, 0) + prv(w, 0) + nxt(w, 1) + prv(w, 1)
                w = w + kappa * (near - 4.0 * w)
            w = w[PAD:PAD + rows, LANES:LANES + CHUNK]
            if c > 0:
                out[0, f, :, pl.ds(begin, CHUNK)] = w
            else:
                out[0, f, :, pl.ds(cols - LANES, LANES)] = w[:, :LANES]
                out[0, f, :, pl.ds(0, CHUNK - LANES)] = w[:, LANES:]

    def edge_terms(c):
        take_halo(c + 1)
        terms("top", c)
        terms("bottom", c)

    def edge_join(c):
        join("top", c)
        join("bottom", c)

    terms("inner", 0)
    for c in range(1, nch):
        terms("inner", c)
        join("inner", c - 1)
    take_halo(0)
    edge_terms(0)
    join("inner", nch - 1)
    for c in range(1, nch):
        edge_terms(c)
        edge_join(c - 1)
    edge_join(nch - 1)
    for c in range(nch):
        finish("inner", c)
    for c in range(nch):
        finish("top", c)
        finish("bottom", c)
        send_mixed(c)
        if c >= 2:
            take_mixed(c - 1)
            if c == 2:
                take_mixed(0)
            diffuse(c - 1)
    take_mixed(nch - 1)
    if nch == 2:
        take_mixed(0)
    diffuse(nch - 1)
    diffuse(0)

    for c in range(nch):
        for name in blocks:
            for k in range(pairs):
                a_copy(name, c, k).wait_send()
                if k > 0:
                    b_copy(name, c, k).wait_send()

    @pl.when(has_down)
    def _():
        for piece in range(nch + 1):
            for copy in to_down(piece):
                copy.wait_send()
        for c in range(nch):
            m_copy(0, c).wait_send()

    @pl.when(has_up)
    def _():
        for piece in range(nch + 1):
            for copy in to_up(piece):
                copy.wait_send()
        for c in range(nch):
            m_copy(1, c).wait_send()


def solution(mesh):
    subs, tiles = mesh.shape["sub"], mesh.shape["tile"]

    def local(states, terrain, depth_table, spread_table, mixing):
        _, fields, rows, cols = states.shape
        pairs = subs // 2
        nch = cols // CHUNK
        tall = rows + 2 * PAD
        dma = pltpu.SemaphoreType.DMA
        many = max(pairs - 1, 1)
        return pl.pallas_call(
            functools.partial(kernel, subs, tiles, rows, cols, depth_table.shape[0]),
            out_shape=jax.ShapeDtypeStruct(states.shape, jnp.float32),
            in_specs=[pl.BlockSpec(memory_space=pltpu.HBM)] * 5,
            out_specs=pl.BlockSpec(memory_space=pltpu.VMEM),
            scratch_shapes=[
                pltpu.SMEM(depth_table.shape, jnp.float32),
                pltpu.SMEM(spread_table.shape, jnp.float32),
                pltpu.SMEM(mixing.shape, jnp.float32),
                pltpu.VMEM((fields, tall, cols), jnp.float32),
                pltpu.VMEM((tall, cols), jnp.int32),
                pltpu.VMEM((tall, cols), jnp.float32),
                pltpu.VMEM((tall, cols), jnp.float32),
                pltpu.VMEM((pairs, fields, rows, cols), jnp.float32),
                pltpu.VMEM((pairs, fields, rows, cols), jnp.float32),
                pltpu.VMEM((many, fields, rows, cols), jnp.float32),
                pltpu.VMEM((many, fields, rows, cols), jnp.float32),
                pltpu.VMEM((fields, tall, cols), jnp.float32),
                dma((5,)),
                dma((4, nch + 1)),
                dma((4, nch + 1)),
                dma((pairs, 3, nch)),
                dma((pairs, 3, nch)),
                dma((many, 3, nch)),
                dma((many, 3, nch)),
                dma((2, nch)),
                dma((2, nch)),
            ],
            compiler_params=pltpu.CompilerParams(
                collective_id=0, has_side_effects=True, vmem_limit_bytes=48 * 1024 * 1024
            ),
            name="gradient",
        )(*(pltpu.with_memory_space_constraint(value, pltpu.HBM) for value in (states, terrain, depth_table, spread_table, mixing)))

    in_specs = (P("sub", None, "tile", None), P("tile", None), P(), P(), P())
    out_specs = P("sub", None, "tile", None)
    return jax.shard_map(local, mesh=mesh, in_specs=in_specs, out_specs=out_specs, check_vma=False)
```

```python
import functools

import jax
import jax.numpy as jnp
from jax import lax
from jax.experimental import pallas as pl
from jax.experimental.pallas import tpu as pltpu
from jax.sharding import PartitionSpec as P

FSTEPS = 3
DSTEPS = 3
time_step = 0.5
gravity = 1.0
coriolis = 0.3

PAD = 8
LANES = 128
FHALO = 2 * FSTEPS
CHUNK = 512


def kernel(
    subs, tiles, rows, cols, nclass,
    states, terrain, depth_in, spread_in, mixing_in, out,
    depth_tab, spread_tab, mixing, S, T, D, K, send_a, recv_a, send_b, recv_b, M,
    load_sem, halo_send, halo_recv, a_send, a_recv, b_send, b_recv, m_send, m_recv,
):
    pairs = subs // 2
    nch = cols // CHUNK
    me = lax.axis_index("sub")
    tile = lax.axis_index("tile")
    parity = lax.rem(me, 2)
    mate = me + 1 - 2 * parity
    pair = me // 2
    has_up = tile > 0
    has_down = tile < tiles - 1
    up, down = tile - 1, tile + 1

    loads = [
        pltpu.make_async_copy(states.at[0], S.at[:, pl.ds(PAD, rows), :], load_sem.at[0]),
        pltpu.make_async_copy(terrain, T.at[pl.ds(PAD, rows), :], load_sem.at[1]),
        pltpu.make_async_copy(depth_in, depth_tab, load_sem.at[2]),
        pltpu.make_async_copy(spread_in, spread_tab, load_sem.at[3]),
        pltpu.make_async_copy(mixing_in, mixing, load_sem.at[4]),
    ]
    for copy in loads:
        copy.start()

    barrier = pltpu.get_barrier_semaphore()
    pl.semaphore_signal(barrier, inc=1, device_id={"sub": mate})
    for k in range(1, pairs):
        pl.semaphore_signal(
            barrier, inc=1, device_id={"sub": lax.rem(pair + k, pairs) * 2 + parity}
        )

    @pl.when(has_up)
    def _():
        pl.semaphore_signal(barrier, inc=1, device_id={"tile": up})

    @pl.when(has_down)
    def _():
        pl.semaphore_signal(barrier, inc=1, device_id={"tile": down})

    pl.semaphore_wait(
        barrier, pairs + has_up.astype(jnp.int32) + has_down.astype(jnp.int32)
    )

    def halo_copy(source, target, index, where):
        return pltpu.make_async_remote_copy(
            src_ref=source, dst_ref=target, send_sem=halo_send.at[index[0], index[1]],
            recv_sem=halo_recv.at[index[0], index[1]], device_id={"tile": where},
            device_id_type=pl.DeviceIdType.MESH,
        )

    last, first = pl.ds(rows - FHALO, FHALO), pl.ds(0, FHALO)
    above, below = pl.ds(PAD - FHALO, FHALO), pl.ds(PAD + rows, FHALO)
    spans = [(cols - LANES, LANES)]
    for c in range(nch):
        begin = c * CHUNK + LANES if c > 0 else 0
        spans.append((begin, min((c + 1) * CHUNK + LANES, cols - LANES) - begin))

    def to_down(piece):
        at = pl.ds(*spans[piece])
        return [
            halo_copy(terrain.at[last, at], T.at[above, at], (0, piece), down),
            halo_copy(states.at[0, :, last, at], S.at[:, above, at], (1, piece), down),
        ]

    def to_up(piece):
        at = pl.ds(*spans[piece])
        return [
            halo_copy(terrain.at[first, at], T.at[below, at], (2, piece), up),
            halo_copy(states.at[0, :, first, at], S.at[:, below, at], (3, piece), up),
        ]

    for piece in range(nch + 1):

        @pl.when(has_down)
        def _():
            for copy in to_down(piece):
                copy.start()

        @pl.when(has_up)
        def _():
            for copy in to_up(piece):
                copy.start()

    S[:, 0:PAD - FHALO, :] = jnp.zeros((3, PAD - FHALO, cols), jnp.float32)
    T[0:PAD - FHALO, :] = jnp.full((PAD - FHALO, cols), -1, jnp.int32)
    S[:, PAD + rows + FHALO:, :] = jnp.zeros((3, PAD - FHALO, cols), jnp.float32)
    T[PAD + rows + FHALO:, :] = jnp.full((PAD - FHALO, cols), -1, jnp.int32)
    M[:, 0:PAD - DSTEPS, :] = jnp.zeros((3, PAD - DSTEPS, cols), jnp.float32)
    M[:, PAD + rows + DSTEPS:, :] = jnp.zeros((3, PAD - DSTEPS, cols), jnp.float32)

    @pl.when(jnp.logical_not(has_up))
    def _():
        S[:, PAD - FHALO:PAD, :] = jnp.zeros((3, FHALO, cols), jnp.float32)
        T[PAD - FHALO:PAD, :] = jnp.full((FHALO, cols), -1, jnp.int32)
        M[:, PAD - DSTEPS:PAD, :] = jnp.zeros((3, DSTEPS, cols), jnp.float32)

    @pl.when(jnp.logical_not(has_down))
    def _():
        S[:, PAD + rows:PAD + rows + FHALO, :] = jnp.zeros((3, FHALO, cols), jnp.float32)
        T[PAD + rows:PAD + rows + FHALO, :] = jnp.full((FHALO, cols), -1, jnp.int32)
        M[:, PAD + rows:PAD + rows + DSTEPS, :] = jnp.zeros((3, DSTEPS, cols), jnp.float32)

    def lookup(start, count, begin, width):
        at = (pl.ds(start, count), pl.ds(begin, width))
        kind = T[at]
        depth = jnp.zeros(kind.shape, jnp.float32)
        kappa = jnp.zeros(kind.shape, jnp.float32)
        for n in range(nclass):
            hit = kind == n
            depth = jnp.where(hit, depth_tab[n], depth)
            kappa = jnp.where(hit, spread_tab[n], kappa)
        D[at] = depth
        K[at] = kappa

    def take_halo(piece):
        @pl.when(has_up)
        def _():
            for copy in to_down(piece):
                copy.wait_recv()

        @pl.when(has_down)
        def _():
            for copy in to_up(piece):
                copy.wait_recv()

        lookup(0, PAD, *spans[piece])
        lookup(PAD + rows, PAD, *spans[piece])

    for copy in loads:
        copy.wait()
    for c in range(nch):
        lookup(PAD, rows, c * CHUNK, CHUNK)

    def wide(ref, lead, start, count, begin):
        begin, width = (begin - LANES) % cols, CHUNK + 2 * LANES
        parts = []
        while width > 0:
            size = min(width, cols - begin)
            parts.append(ref[lead + (pl.ds(start, count), pl.ds(begin, size))])
            begin, width = (begin + size) % cols, width - size
        return parts[0] if len(parts) == 1 else jnp.concatenate(parts, axis=-1)

    def nxt(value, axis):
        return pltpu.roll(value, value.shape[axis] - 1, axis)

    def prv(value, axis):
        return pltpu.roll(value, 1, axis)

    def diff(value, axis):
        return nxt(value, axis) - prv(value, axis)

    def forward(start, count, c, masked):
        h, u, v = (wide(S, (f,), start, count, c * CHUNK) for f in range(3))
        d = wide(D, (), start, count, c * CHUNK)
        if masked:
            index = (
                tile * rows - PAD + start + lax.broadcasted_iota(jnp.int32, h.shape, 0)
            )
            inside = (index >= 0) & (index < tiles * rows)
        for _ in range(FSTEPS):
            new_h = h - (time_step * 0.5) * (diff(d * u, 0) + diff(d * v, 1))
            if masked:
                new_h = jnp.where(inside, new_h, 0.0)
            new_u = u - (time_step * gravity * 0.5) * diff(new_h, 0) + (time_step * coriolis) * v
            new_v = v - (time_step * gravity * 0.5) * diff(new_h, 1) - (time_step * coriolis) * u
            h, u, v = new_h, new_u, new_v
        return h, u, v

    later = jnp.minimum(me + 1, subs - 1)
    keep = jnp.where(me < subs - 1, 1.0, 0.0)

    def weights(s):
        return mixing[s, me], mixing[s, later] * keep

    dest_pair = [lax.rem(pair + k, pairs) for k in range(pairs)]
    w_mine = [weights(q * 2 + parity) for q in dest_pair]
    w_mate = [weights(q * 2 + 1 - parity) for q in dest_pair]

    edge = PAD
    inner = rows - 2 * edge
    blocks = {
        "inner": (edge, inner),
        "top": (0, edge),
        "bottom": (rows - edge, edge),
    }
    numbers = {"inner": 0, "top": 1, "bottom": 2}

    def a_copy(name, c, k):
        row, count = blocks[name]
        at = (k, slice(None), pl.ds(row, count), pl.ds(c * CHUNK, CHUNK))
        return pltpu.make_async_remote_copy(
            src_ref=send_a.at[at], dst_ref=recv_a.at[at],
            send_sem=a_send.at[k, numbers[name], c], recv_sem=a_recv.at[k, numbers[name], c],
            device_id={"sub": mate}, device_id_type=pl.DeviceIdType.MESH,
        )

    def b_copy(name, c, k):
        row, count = blocks[name]
        at = (k - 1, slice(None), pl.ds(row, count), pl.ds(c * CHUNK, CHUNK))
        return pltpu.make_async_remote_copy(
            src_ref=send_b.at[at], dst_ref=recv_b.at[at],
            send_sem=b_send.at[k - 1, numbers[name], c],
            recv_sem=b_recv.at[k - 1, numbers[name], c],
            device_id={"sub": dest_pair[k] * 2 + parity},
            device_id_type=pl.DeviceIdType.MESH,
        )

    def terms(name, c):
        row, count = blocks[name]
        if name == "inner":
            ends = forward(PAD, rows, c, False)
            skip = edge
        else:
            ends = forward(row, PAD + edge + PAD, c, True)
            skip = PAD
        span = pl.ds(c * CHUNK, CHUNK)
        order = list(range(1, pairs)) + [0]
        for k in order:
            for f in range(3):
                end = ends[f][skip:skip + count, LANES:LANES + CHUNK]
                start = S[f, pl.ds(PAD + row, count), span]
                a, b = w_mate[k]
                send_a[k, f, pl.ds(row, count), span] = a * start - b * end
                a, b = w_mine[k]
                mine = a * start - b * end
                if k == 0:
                    M[f, pl.ds(PAD + row, count), span] = mine
                else:
                    send_b[k - 1, f, pl.ds(row, count), span] = mine
            a_copy(name, c, k).start()

    def join(name, c):
        row, count = blocks[name]
        span = pl.ds(c * CHUNK, CHUNK)
        for k in list(range(1, pairs)) + [0]:
            a_copy(name, c, k).wait_recv()
            for f in range(3):
                got = recv_a[k, f, pl.ds(row, count), span]
                if k == 0:
                    at = (f, pl.ds(PAD + row, count), span)
                    M[at] = M[at] + got
                else:
                    at = (k - 1, f, pl.ds(row, count), span)
                    send_b[at] = send_b[at] + got
            if k > 0:
                b_copy(name, c, k).start()

    def finish(name, c):
        row, count = blocks[name]
        span = pl.ds(c * CHUNK, CHUNK)
        for k in range(1, pairs):
            b_copy(name, c, k).wait_recv()
        for f in range(3):
            at = (f, pl.ds(PAD + row, count), span)
            total = M[at]
            for k in range(1, pairs):
                total = total + recv_b[k - 1, f, pl.ds(row, count), span]
            M[at] = total

    def m_copy(way, c):
        span = pl.ds(c * CHUNK, CHUNK)
        if way == 0:
            source, target, where = pl.ds(PAD + rows - DSTEPS, DSTEPS), pl.ds(PAD - DSTEPS, DSTEPS), down
        else:
            source, target, where = pl.ds(PAD, DSTEPS), pl.ds(PAD + rows, DSTEPS), up
        return pltpu.make_async_remote_copy(
            src_ref=M.at[:, source, span], dst_ref=M.at[:, target, span],
            send_sem=m_send.at[way, c], recv_sem=m_recv.at[way, c],
            device_id={"tile": where}, device_id_type=pl.DeviceIdType.MESH,
        )

    def send_mixed(c):
        @pl.when(has_down)
        def _():
            m_copy(0, c).start()

        @pl.when(has_up)
        def _():
            m_copy(1, c).start()

    def take_mixed(c):
        @pl.when(has_up)
        def _():
            m_copy(0, c).wait_recv()

        @pl.when(has_down)
        def _():
            m_copy(1, c).wait_recv()

    def diffuse(c):
        begin = c * CHUNK - LANES
        total = rows + 2 * PAD
        kappa = wide(K, (), 0, total, begin)
        for f in range(3):
            w = wide(M, (f,), 0, total, begin)
            for _ in range(DSTEPS):
                near = nxt(w, 0) + prv(w, 0) + nxt(w, 1) + prv(w, 1)
                w = w + kappa * (near - 4.0 * w)
            w = w[PAD:PAD + rows, LANES:LANES + CHUNK]
            if c > 0:
                out[0, f, :, pl.ds(begin, CHUNK)] = w
            else:
                out[0, f, :, pl.ds(cols - LANES, LANES)] = w[:, :LANES]
                out[0, f, :, pl.ds(0, CHUNK - LANES)] = w[:, LANES:]

    def edge_terms(c):
        take_halo(c + 1)
        terms("top", c)
        terms("bottom", c)

    def edge_join(c):
        join("top", c)
        join("bottom", c)

    terms("inner", 0)
    for c in range(1, nch):
        terms("inner", c)
        join("inner", c - 1)
    take_halo(0)
    edge_terms(0)
    join("inner", nch - 1)
    for c in range(1, nch):
        edge_terms(c)
        edge_join(c - 1)
        finish("inner", c - 1)
    edge_join(nch - 1)
    finish("inner", nch - 1)
    for c in range(nch):
        finish("top", c)
        finish("bottom", c)
        send_mixed(c)
        if c >= 2:
            take_mixed(c - 1)
            if c == 2:
                take_mixed(0)
            diffuse(c - 1)
    take_mixed(nch - 1)
    if nch == 2:
        take_mixed(0)
    diffuse(nch - 1)
    diffuse(0)

    for c in range(nch):
        for name in blocks:
            for k in range(pairs):
                a_copy(name, c, k).wait_send()
                if k > 0:
                    b_copy(name, c, k).wait_send()

    @pl.when(has_down)
    def _():
        for piece in range(nch + 1):
            for copy in to_down(piece):
                copy.wait_send()
        for c in range(nch):
            m_copy(0, c).wait_send()

    @pl.when(has_up)
    def _():
        for piece in range(nch + 1):
            for copy in to_up(piece):
                copy.wait_send()
        for c in range(nch):
            m_copy(1, c).wait_send()


def solution(mesh):
    subs, tiles = mesh.shape["sub"], mesh.shape["tile"]

    def local(states, terrain, depth_table, spread_table, mixing):
        _, fields, rows, cols = states.shape
        pairs = subs // 2
        nch = cols // CHUNK
        tall = rows + 2 * PAD
        dma = pltpu.SemaphoreType.DMA
        many = max(pairs - 1, 1)
        return pl.pallas_call(
            functools.partial(kernel, subs, tiles, rows, cols, depth_table.shape[0]),
            out_shape=jax.ShapeDtypeStruct(states.shape, jnp.float32),
            in_specs=[pl.BlockSpec(memory_space=pltpu.HBM)] * 5,
            out_specs=pl.BlockSpec(memory_space=pltpu.VMEM),
            scratch_shapes=[
                pltpu.SMEM(depth_table.shape, jnp.float32),
                pltpu.SMEM(spread_table.shape, jnp.float32),
                pltpu.SMEM(mixing.shape, jnp.float32),
                pltpu.VMEM((fields, tall, cols), jnp.float32),
                pltpu.VMEM((tall, cols), jnp.int32),
                pltpu.VMEM((tall, cols), jnp.float32),
                pltpu.VMEM((tall, cols), jnp.float32),
                pltpu.VMEM((pairs, fields, rows, cols), jnp.float32),
                pltpu.VMEM((pairs, fields, rows, cols), jnp.float32),
                pltpu.VMEM((many, fields, rows, cols), jnp.float32),
                pltpu.VMEM((many, fields, rows, cols), jnp.float32),
                pltpu.VMEM((fields, tall, cols), jnp.float32),
                dma((5,)),
                dma((4, nch + 1)),
                dma((4, nch + 1)),
                dma((pairs, 3, nch)),
                dma((pairs, 3, nch)),
                dma((many, 3, nch)),
                dma((many, 3, nch)),
                dma((2, nch)),
                dma((2, nch)),
            ],
            compiler_params=pltpu.CompilerParams(
                collective_id=0, has_side_effects=True, vmem_limit_bytes=48 * 1024 * 1024
            ),
            name="gradient",
        )(*(pltpu.with_memory_space_constraint(value, pltpu.HBM) for value in (states, terrain, depth_table, spread_table, mixing)))

    in_specs = (P("sub", None, "tile", None), P("tile", None), P(), P(), P())
    out_specs = P("sub", None, "tile", None)
    return jax.shard_map(local, mesh=mesh, in_specs=in_specs, out_specs=out_specs, check_vma=False)
```
